32 devices in a mesh: member: 1, lat: 4 (over z), lev: 4 (over y, x), fld: 2 (over core).
Axes of the slice: x: 2, y: 2, z: 4, core: 2. Of those that a mesh axis runs over, the one named last changes fastest.
Arguments:
- grid_state: bfloat16 [2, 16, 2, 512, 2048], P('member', 'lev', 'fld', 'lat'), may hold values from -6 to 6
- legendre: bfloat16 [512, 2, 512, 640], P(('lat', 'lev'), 'fld'), may hold values from -0.25 to 0.25
- pair_order: int32 [512], replicated, may hold values from 0 to 511, each once
- band_start: int32 [1024], replicated, may hold values from 0 to 286
- mode_analysis: float32 [32, 32], replicated, may hold values from -1 to 1
- mode_synthesis: float32 [32, 32], replicated, may hold values from -1 to 1
- mode_rate: float32 [32], replicated, may hold values from 0.05 to 50
Outputs:
- grid_out: bfloat16 [2, 16, 2, 512, 2048], P('member', 'lev', 'fld', 'lat')
The draws below stay inside these ranges and needn't reach their ends.
Inputs may be any that keep to these rules, and one draw needn't show every extreme that they name: `pair_order`: every value appears once.
All inputs are finite; a program needn't handle non-finite values.
Results may differ from the reference program's by a relative error of at most 0.009.
Values may be sent and summed in bfloat16 or wider, within the bound.
No kernel may reach another device: no remote copies, remote signals or barrier semaphores. Data moves between devices by JAX's collectives and lax.ppermute only.
A program may use at most 128 MiB of HBM per device.

```python
import math
import jax
import jax.numpy as jnp
from jax import lax

M = 1024
LEVELS = 16
FIELDS = 2
HLAT = 512
NLON = 2048
PAIRS = 512
COLS = 640
MODES = 32


def draw_band_start(key, part):
    wave_list = jnp.arange(M, dtype=jnp.int32)
    spread = jax.random.randint(key, (M,), 0, HLAT // 16, dtype=jnp.int32)
    spread = jnp.where(wave_list == 0, 0, jnp.where(wave_list == M - 1, HLAT // 16 - 1, spread))
    return (wave_list * (HLAT // 2) // M + spread).astype(jnp.int32)


def levels(stream_key, shape, pieces, least, largest):
    def one(axis_at, shards_of):
        steps = jax.random.uniform(jax.random.fold_in(jax.random.fold_in(stream_key, 6), axis_at), (shards_of,), jnp.float32, least / len(pieces), largest / len(pieces))
        return jnp.repeat(jnp.exp(steps), shape[axis_at] // shards_of).reshape((-1,) + (1,) * (len(shape) - axis_at - 1))

    level = one(*pieces[0])
    for cut in pieces[1:]:
        level = level * one(*cut)
    return level


def gaussian(key, shape, deviation, most, shards=(), kind=jnp.bfloat16):
    loudness = levels(key, shape, shards, -0.22, 0.18) if shards else 1.0
    entries = jax.random.normal(key, shape, jnp.float32) * deviation * loudness
    return jnp.minimum(jnp.maximum(entries, -most), most).astype(kind)


def setup_inputs(seed: int = 0, part: int = 0) -> dict:
    streams_of = jax.random.split(jax.random.key(seed), 8)
    own_keys = jax.random.split(jax.random.fold_in(streams_of[7], part), 8)
    grid_state = gaussian(own_keys[0], (2, LEVELS, 2, HLAT, NLON), 1.0, 6.0, ((1, 4), (2, 2), (3, 4)))
    legendre = gaussian(streams_of[1], (PAIRS, 2, HLAT, COLS), HLAT ** -0.5, 0.25, ((0, 16), (1, 2)))
    pair_order = jax.random.permutation(streams_of[2], PAIRS).astype(jnp.int32)
    band_start = draw_band_start(jax.random.fold_in(streams_of[7], 71), part)
    mode_analysis = gaussian(streams_of[4], (MODES, MODES), MODES ** -0.5, 1.0, (), jnp.float32)
    mode_synthesis = gaussian(streams_of[5], (MODES, MODES), MODES ** -0.5, 1.0, (), jnp.float32)
    mode_rate = jnp.clip(jnp.exp(jax.random.uniform(streams_of[6], (MODES,), jnp.float32, math.log(0.05), math.log(50.0))), 0.05, 50.0)
    return {"grid_state": grid_state, "legendre": legendre, "pair_order": pair_order, "band_start": band_start, "mode_analysis": mode_analysis, "mode_synthesis": mode_synthesis, "mode_rate": mode_rate}


def fourier_table(wave_list, lon_count):
    longitude = jnp.arange(lon_count, dtype=jnp.int32)
    phase = longitude[:, None] * wave_list[None, :] % lon_count
    angle = phase.astype(jnp.float32) * jnp.float32(2.0 * math.pi / lon_count)
    scaling = jnp.float32(1.0 / math.sqrt(lon_count))
    return jnp.stack([jnp.cos(angle) * scaling, -jnp.sin(angle) * scaling], axis=1).astype(jnp.bfloat16)

def column_maps(first_wave, parity, wave_count, col_count):
    column = jnp.arange(col_count, dtype=jnp.int32)[None, :]
    first_col = first_wave[:, None]
    second_col = wave_count - 1 - first_col
    count_one = (wave_count - 1 - first_col - parity) // 2 + 1
    count_two = jnp.maximum((first_col - parity) // 2 + 1, 0)
    in_first = column < count_one
    degree = jnp.where(in_first, first_col + parity + 2 * column, second_col + parity + 2 * (column - count_one))
    valid = column < count_one + count_two
    return (in_first, degree, valid)

def mode_factor(degree, mode_rate, wave_count):
    level_deg = degree.astype(jnp.float32)
    growth = level_deg * (level_deg + 1.0) / float(wave_count * wave_count)
    return 1.0 / (1.0 + growth[..., None, :] * mode_rate[:, None])

def reference(grid_state, legendre, pair_order, band_start, mode_analysis, mode_synthesis, mode_rate):
    wind_part = grid_state[0].astype(jnp.float32)
    heat_part = grid_state[1].astype(jnp.float32)
    products = jnp.stack([wind_part * heat_part, wind_part * wind_part - heat_part * heat_part]).astype(jnp.bfloat16)
    products = lax.optimization_barrier(products)
    wave_list = jnp.arange(M, dtype=jnp.int32)
    lon_table = fourier_table(wave_list, NLON)
    grid_rows = products.reshape(-1, NLON).astype(jnp.float32)
    fourier = jnp.dot(grid_rows, lon_table.reshape(NLON, 2 * M).astype(jnp.float32)).astype(jnp.bfloat16)
    fourier = lax.optimization_barrier(fourier)
    fourier = fourier.reshape(FIELDS, LEVELS, 2, HLAT, 2, M).astype(jnp.float32)
    halves = jnp.stack([fourier[:, :, 0] + fourier[:, :, 1], fourier[:, :, 0] - fourier[:, :, 1]]).astype(jnp.bfloat16)
    halves = lax.optimization_barrier(halves)
    by_wave = jnp.transpose(halves, (5, 0, 4, 1, 2, 3))
    latitude = jnp.arange(HLAT, dtype=jnp.int32)

    def one_slot(slot_item):
        slot_table, first_wave = slot_item
        second_wave = M - 1 - first_wave
        results = []
        for parity in range(2):
            in_first, degree, valid = column_maps(first_wave[None], parity, M, COLS)
            start_col = jnp.where(in_first[0], band_start[first_wave], band_start[second_wave])
            keep_mask = valid[0][None, :] & (latitude[:, None] >= start_col[None, :])
            active = jnp.where(keep_mask, slot_table[parity], jnp.zeros((), jnp.bfloat16)).astype(jnp.float32)
            first_part = by_wave[first_wave, parity].astype(jnp.float32)
            second_part = by_wave[second_wave, parity].astype(jnp.float32)
            spec_one = jnp.einsum('eflj,jc->eflc', first_part, active)
            spec_two = jnp.einsum('eflj,jc->eflc', second_part, active)
            spectral = jnp.where(in_first[0], spec_one, spec_two).reshape(2, MODES, COLS)
            mixed = jnp.einsum('ki,eic->ekc', mode_analysis, spectral, precision=lax.Precision.HIGHEST)
            factor = mode_factor(degree, mode_rate, M)[0]
            coupled = jnp.einsum('ik,ekc->eic', mode_synthesis, mixed * factor[None], precision=lax.Precision.HIGHEST)
            coupled = lax.optimization_barrier(coupled.astype(jnp.bfloat16)).astype(jnp.float32)
            coupled = coupled.reshape(2, FIELDS, LEVELS, COLS)
            pick_first = in_first[0].astype(jnp.float32)
            back_one = jnp.einsum('jc,eflc->eflj', active, coupled * pick_first)
            back_two = jnp.einsum('jc,eflc->eflj', active, coupled * (1.0 - pick_first))
            results.append(jnp.stack([back_one, back_two]))
        return jnp.stack(results).astype(jnp.bfloat16)
    per_slot = lax.map(one_slot, (legendre, pair_order))
    slot_of = jnp.zeros((PAIRS,), jnp.int32).at[pair_order].set(jnp.arange(PAIRS, dtype=jnp.int32))
    low_half = per_slot[slot_of][:, :, 0]
    high_half = per_slot[slot_of[::-1]][:, :, 1]
    back_waves = jnp.concatenate([low_half, high_half], axis=0).astype(jnp.float32)
    north_half = back_waves[:, 0] + back_waves[:, 1]
    south_half = back_waves[:, 0] - back_waves[:, 1]
    hemi_grid = jnp.stack([north_half, south_half], axis=0).astype(jnp.bfloat16)
    hemi_grid = lax.optimization_barrier(hemi_grid)
    hemi_grid = jnp.transpose(hemi_grid, (3, 4, 0, 5, 2, 1))
    weight = jnp.where(wave_list == 0, 1.0, 2.0).astype(jnp.float32)
    inverse = (lon_table.astype(jnp.float32) * weight[None, None, :]).astype(jnp.bfloat16)
    grid_out = jnp.dot(hemi_grid.reshape(-1, 2 * M).astype(jnp.float32), inverse.reshape(NLON, 2 * M).astype(jnp.float32).T)
    return grid_out.astype(jnp.bfloat16).reshape(FIELDS, LEVELS, 2, HLAT, NLON)
```

```python
import functools
import math

import jax
import jax.numpy as jnp
from jax import lax
from jax.experimental import pallas as pl
from jax.experimental.pallas import tpu as pltpu
from jax.sharding import PartitionSpec as P


LANES = 128


def swap_with(value, axis, mask):
    if mask == 0:
        return value
    pairs = [(source, source ^ mask) for source in range(lax.axis_size(axis))]
    return lax.ppermute(value, axis, pairs)


def pick(table, index):
    places = jnp.arange(table.shape[0], dtype=jnp.int32)
    return jnp.sum(jnp.where(index[:, None] == places[None, :], table[None, :], 0), axis=1)


def table_kernel(fine_cos, fine_sin, coarse_cos, coarse_sin, out):
    rows = out.shape[2]
    for block in range(out.shape[0]):
        here = slice(block * rows, (block + 1) * rows)
        c_fine, s_fine = fine_cos[here, :], fine_sin[here, :]
        for part in range(coarse_cos.shape[1]):
            c_coarse = coarse_cos[here, part : part + 1]
            s_coarse = coarse_sin[here, part : part + 1]
            there = slice(part * LANES, (part + 1) * LANES)
            out[block, 0, :, there] = (c_coarse * c_fine - s_coarse * s_fine).astype(out.dtype)
            out[block, 1, :, there] = -(s_coarse * c_fine + c_coarse * s_fine).astype(out.dtype)


def small_tables(waves, lon_count):
    fine = jnp.arange(LANES, dtype=jnp.int32)
    coarse = jnp.arange(lon_count // LANES, dtype=jnp.int32) * LANES
    turn = jnp.float32(2.0 * math.pi / lon_count)
    scaling = jnp.float32(1.0 / math.sqrt(lon_count))
    a_fine = (waves[:, None] * fine[None, :] % lon_count).astype(jnp.float32) * turn
    a_coarse = (waves[:, None] * coarse[None, :] % lon_count).astype(jnp.float32) * turn
    return (
        jnp.cos(a_fine) * scaling,
        jnp.sin(a_fine) * scaling,
        jnp.cos(a_coarse),
        jnp.sin(a_coarse),
    )


def expand_table(smalls, blocks, rows, lon_count):
    step = 4 if blocks % 4 == 0 else 1
    height = step * rows
    coarse = lon_count // LANES
    return pl.pallas_call(
        table_kernel,
        grid=(blocks // step,),
        in_specs=[
            pl.BlockSpec((height, LANES), lambda i: (i, 0)),
            pl.BlockSpec((height, LANES), lambda i: (i, 0)),
            pl.BlockSpec((height, coarse), lambda i: (i, 0)),
            pl.BlockSpec((height, coarse), lambda i: (i, 0)),
        ],
        out_specs=pl.BlockSpec((step, 2, rows, lon_count), lambda i: (i, 0, 0, 0)),
        out_shape=jax.ShapeDtypeStruct((blocks, 2, rows, lon_count), jnp.bfloat16),
        cost_estimate=pl.CostEstimate(
            flops=blocks * rows * lon_count * 6,
            bytes_accessed=blocks * rows * lon_count * 4,
            transcendentals=0,
        ),
    )(*smalls)


def legendre_kernel(numbers, *refs, lats, lat_blocks, lev_count, wave_count, slots):
    pieces, (table, analysis, synthesis, rate, out, work) = refs[:lev_count], refs[lev_count:]
    slot = pl.program_id(0)
    lines = pieces[0].shape[3] // lats
    rows = 2 * lev_count * lines
    tall = 2 * slots

    def place(dist, part, lev, line):
        return pl.ds(((dist * 2 + part) * lev_count * lines + lev * lines + line) * tall, tall)

    @pl.when(slot == 0)
    def _():
        for dist in range(lat_blocks):
            for part in range(2):
                for lev in range(lev_count):
                    for line in range(lines):
                        work[place(dist, part, lev, line), :] = pieces[lev][
                            dist, part, :, line * lats : (line + 1) * lats
                        ].astype(jnp.float32)

    parity = numbers[lat_blocks]
    first = numbers[lat_blocks + 1 + slot]
    starts = [numbers[lat_blocks + 1 + slots + slot], numbers[lat_blocks + 1 + 2 * slots + slot]]
    second = wave_count - 1 - first
    count_one = (wave_count - 1 - first - parity) // 2 + 1
    count_two = jnp.where(first >= parity, (first - parity) // 2 + 1, 0)
    cols = table.shape[3]
    column = lax.broadcasted_iota(jnp.int32, (1, cols), 1)
    in_first = column < count_one
    in_second = (column >= count_one) & (column < count_one + count_two)
    degree = jnp.where(
        in_first, first + parity + 2 * column, second + parity + 2 * (column - count_one)
    )
    lane = lax.broadcasted_iota(jnp.int32, (1, lats), 1)

    both = jnp.zeros((2 * rows, cols), jnp.float32)
    for dist in range(lat_blocks):
        block = numbers[dist]
        values = []
        for which in range(2):
            at = dist * rows * tall + 2 * slot + which
            value = work[pl.ds(at, rows, stride=tall), :]
            keep = lane + block * lats >= starts[which]
            values.append(jnp.where(keep, value, 0.0))
        value = jnp.concatenate(values, axis=0).astype(jnp.bfloat16)
        here = pl.ds(pl.multiple_of(block * lats, lats), lats)
        both = both + jnp.dot(value, table[0, 0, here, :], preferred_element_type=jnp.float32)
    spectral = jnp.where(in_first, both[:rows], both[rows:])
    level_deg = degree.astype(jnp.float32)
    growth = level_deg * (level_deg + 1.0) / float(wave_count * wave_count)
    factor = 1.0 / (1.0 + growth * rate[...])
    mixed = jnp.dot(
        analysis[...], spectral, precision=lax.Precision.HIGHEST, preferred_element_type=jnp.float32
    )
    coupled = jnp.dot(
        synthesis[...],
        mixed * factor,
        precision=lax.Precision.HIGHEST,
        preferred_element_type=jnp.float32,
    )
    split = jnp.concatenate(
        [jnp.where(in_first, coupled, 0.0), jnp.where(in_second, coupled, 0.0)], axis=0
    ).astype(jnp.bfloat16)
    for dist in range(lat_blocks):
        block = numbers[dist]
        here = pl.ds(pl.multiple_of(block * lats, lats), lats)
        back = lax.dot_general(
            split,
            table[0, 0, here, :],
            (((1,), (1,)), ((), ())),
            preferred_element_type=jnp.float32,
        )
        for which in range(2):
            at = dist * rows * tall + 2 * slot + which
            keep = lane + block * lats >= starts[which]
            work[pl.ds(at, rows, stride=tall), :] = jnp.where(
                keep, back[which * rows : (which + 1) * rows], 0.0
            )

    @pl.when(slot == slots - 1)
    def _():
        for dist in range(lat_blocks):
            for part in range(2):
                for lev in range(lev_count):
                    for line in range(lines):
                        out[lev, dist, part, :, line * lats : (line + 1) * lats] = work[
                            place(dist, part, lev, line), :
                        ].astype(out.dtype)


def legendre_stage(pieces, legendre, numbers, analysis, synthesis, rate, sizes, slots, first_slot):
    lev_count = len(pieces)
    lat_blocks, _, tall, width = pieces[0].shape
    lats = sizes["lats"]
    lat_total, cols = legendre.shape[2:]
    rows = 2 * lev_count * (width // lats)
    whole = lambda shape: pl.BlockSpec(shape, lambda i, n: (0,) * len(shape))
    flops = slots * (2 * 2 * 2 * rows * lat_total * cols + 2 * 2 * 6 * rows * rows * cols)
    return pl.pallas_call(
        functools.partial(
            legendre_kernel,
            lats=lats,
            lat_blocks=lat_blocks,
            lev_count=lev_count,
            wave_count=sizes["waves"],
            slots=slots,
        ),
        grid_spec=pltpu.PrefetchScalarGridSpec(
            num_scalar_prefetch=1,
            grid=(slots,),
            in_specs=[whole(piece.shape) for piece in pieces]
            + [
                pl.BlockSpec((1, 1, lat_total, cols), lambda i, n: (first_slot + i, 0, 0, 0)),
                whole(analysis.shape),
                whole(synthesis.shape),
                whole(rate.shape),
            ],
            out_specs=whole((lev_count,) + pieces[0].shape),
            scratch_shapes=[pltpu.VMEM((lat_blocks * rows * tall, lats), jnp.float32)],
        ),
        out_shape=jax.ShapeDtypeStruct((lev_count,) + pieces[0].shape, jnp.bfloat16),
        cost_estimate=pl.CostEstimate(
            flops=flops,
            bytes_accessed=slots * lat_total * cols * 2 + 4 * lev_count * pieces[0].size,
            transcendentals=0,
        ),
    )(numbers, *pieces, legendre, analysis, synthesis, rate)


def local(grid_state, legendre, pair_order, band_start, mode_analysis, mode_synthesis, mode_rate):
    lat_count = lax.axis_size("lat")
    lev_count = lax.axis_size("lev")
    lat_here = lax.axis_index("lat")
    lev_here = lax.axis_index("lev")
    parity = lax.axis_index("fld")
    wave_count = band_start.shape[0]
    lon_count = grid_state.shape[-1]
    field_count, levels_here, _, lats_here, _ = grid_state.shape
    slots_here = legendre.shape[0]
    modes_count = mode_rate.shape[0]
    width = field_count * levels_here * lats_here
    chunks = math.gcd(slots_here, 4)
    slots = slots_here // chunks
    tall = 2 * slots
    sizes = {"lats": lats_here, "levels": levels_here, "waves": wave_count}

    shape = (chunks, lat_count, lev_count, slots)
    axis = lambda k: lax.broadcasted_iota(jnp.int32, shape, k)
    owner = (axis(1) ^ lat_here) * lev_count + (axis(2) ^ lev_here)
    slot_index = owner * slots_here + axis(0) * slots + axis(3)
    first_waves = pick(pair_order, slot_index.reshape(-1))
    waves = jnp.stack([first_waves, wave_count - 1 - first_waves], axis=1).reshape(-1)
    smalls = small_tables(waves, lon_count)

    own_first = lax.dynamic_slice_in_dim(
        pair_order, (lat_here * lev_count + lev_here) * slots_here, slots_here
    )
    start_one = pick(band_start, own_first)
    start_two = pick(band_start, wave_count - 1 - own_first)
    blocks_at = jnp.arange(lat_count, dtype=jnp.int32) ^ lat_here

    mode_at = (
        jnp.arange(field_count, dtype=jnp.int32)[None, :, None] * (lev_count * levels_here)
        + (jnp.arange(lev_count, dtype=jnp.int32) ^ lev_here)[:, None, None] * levels_here
        + jnp.arange(levels_here, dtype=jnp.int32)[None, None, :]
    ).reshape(-1)
    select = (
        jnp.arange(modes_count, dtype=jnp.int32)[:, None] == mode_at[None, :]
    ).astype(jnp.float32)
    exact = functools.partial(jnp.dot, precision=lax.Precision.HIGHEST)
    part_eye = jnp.eye(2, dtype=jnp.float32)
    analysis = jnp.kron(part_eye, exact(mode_analysis, select))
    synthesis = jnp.kron(part_eye, exact(select.T, mode_synthesis))
    rate = jnp.concatenate([mode_rate, mode_rate])[:, None]

    wind_part = grid_state[0].astype(jnp.float32)
    heat_part = grid_state[1].astype(jnp.float32)
    products = jnp.stack(
        [wind_part * heat_part, wind_part * wind_part - heat_part * heat_part]
    ).astype(jnp.bfloat16)
    grid_rows = products.reshape(-1, lon_count)
    sign_own = (1 - 2 * parity).astype(jnp.float32)

    def combine(partner, own):
        return (partner.astype(jnp.float32) + sign_own * own.astype(jnp.float32)).astype(
            jnp.bfloat16
        )

    chunk_rows = lat_count * lev_count * tall
    tables, incoming = [], []
    for chunk in range(chunks):
        mine = slice(chunk * chunk_rows, (chunk + 1) * chunk_rows)
        table = expand_table(
            [small[mine] for small in smalls], lat_count * lev_count, tall, lon_count
        ).reshape(-1, lon_count)
        tables.append(table)
        fourier = jnp.einsum(
            "nk,rk->nr", table, grid_rows, preferred_element_type=jnp.float32
        ).astype(jnp.bfloat16)
        fourier = fourier.reshape(lat_count, lev_count, 2, tall, width)
        mirror = swap_with(fourier, "fld", 1)
        received = [
            swap_with(combine(mirror[dist], fourier[dist]), "lat", dist)
            for dist in range(lat_count)
        ]
        incoming.append(
            [
                swap_with(jnp.stack([block[dist] for block in received]), "lev", dist)
                for dist in range(lev_count)
            ]
        )
    total = None
    for chunk in range(chunks):
        mine = slice(chunk * slots, (chunk + 1) * slots)
        numbers = jnp.concatenate(
            [blocks_at, parity[None], own_first[mine], start_one[mine], start_two[mine]]
        ).astype(jnp.int32)
        returned = legendre_stage(
            incoming[chunk],
            legendre,
            numbers,
            analysis,
            synthesis,
            rate,
            sizes,
            slots,
            chunk * slots,
        )
        partner = swap_with(returned, "fld", 1)
        own_waves = jnp.stack([own_first[mine], wave_count - 1 - own_first[mine]], axis=1)
        weight = jnp.where(own_waves.reshape(-1) == 0, 1.0, 2.0).astype(jnp.bfloat16)[:, None]
        arrived = [
            swap_with(combine(partner[dist], returned[dist]) * weight, "lev", dist)
            for dist in range(lev_count)
        ]
        hemisphere = jnp.stack(
            [
                swap_with(jnp.stack([block[dist] for block in arrived]), "lat", dist)
                for dist in range(lat_count)
            ]
        ).reshape(-1, width)
        part = jnp.einsum(
            "nr,nk->rk", hemisphere, tables[chunk], preferred_element_type=jnp.float32
        )
        total = part if total is None else total + part
    return total.astype(jnp.bfloat16).reshape(
        field_count, levels_here, 1, lats_here, lon_count
    )


def solution(mesh):
    return jax.shard_map(
        local,
        mesh=mesh,
        in_specs=(
            P("member", "lev", "fld", "lat", None),
            P(("lat", "lev"), "fld", None, None),
            P(),
            P(),
            P(),
            P(),
            P(),
        ),
        out_specs=P("member", "lev", "fld", "lat", None),
        check_vma=False,
    )
```

```python
import functools
import math

import jax
import jax.numpy as jnp
from jax import lax
from jax.experimental import pallas as pl
from jax.experimental.pallas import tpu as pltpu
from jax.sharding import PartitionSpec as P


LANES = 128


def swap_with(value, axis, mask):
    if mask == 0:
        return value
    pairs = [(source, source ^ mask) for source in range(lax.axis_size(axis))]
    return lax.ppermute(value, axis, pairs)


def pick(table, index):
    places = jnp.arange(table.shape[0], dtype=jnp.int32)
    return jnp.sum(jnp.where(index[:, None] == places[None, :], table[None, :], 0), axis=1)


def fold_kernel(state, even, odd):
    half = even.shape[2]
    lats = even.shape[1]
    step = 16 if lats % 16 == 0 else lats

    def products(rows, columns):
        wind_part, heat_part = state[0, 0, 0, rows, columns], state[1, 0, 0, rows, columns]
        wind, heat = wind_part.astype(jnp.float32), heat_part.astype(jnp.float32)
        return wind_part * heat_part, (wind * wind - heat * heat).astype(jnp.bfloat16)

    for top in range(0, lats, step):
        rows = slice(top, top + step)
        for left in range(0, half, LANES):
            columns = slice(left, left + LANES)
            lows = products(rows, columns)
            highs = products(rows, slice(half + left, half + left + LANES))
            for field, (low, high) in enumerate(zip(lows, highs)):
                even[field, rows, columns] = low + high
                odd[field, rows, columns] = low - high


def folded_products(grid_state):
    fields, levels, _, lats, lon_count = grid_state.shape
    half = lon_count // 2
    out = jax.ShapeDtypeStruct((fields, levels * lats, half), jnp.bfloat16)
    even, odd = pl.pallas_call(
        fold_kernel,
        grid=(levels,),
        in_specs=[pl.BlockSpec((fields, 1, 1, lats, lon_count), lambda i: (0, i, 0, 0, 0))],
        out_specs=[pl.BlockSpec((fields, lats, half), lambda i: (0, i, 0))] * 2,
        out_shape=[out, out],
        cost_estimate=pl.CostEstimate(
            flops=grid_state.size * 4, bytes_accessed=grid_state.size * 4, transcendentals=0
        ),
    )(grid_state)
    return even.reshape(-1, half), odd.reshape(-1, half)


def cos_sin(phase, quarter):
    shift = quarter.bit_length() - 1
    quadrant = (phase + quarter // 2) >> shift
    theta = (phase - (quadrant << shift)).astype(jnp.float32) * (0.5 * math.pi / quarter)
    square = theta * theta
    sine = theta * (
        1.0
        + square
        * (-1.0 / 6 + square * (1.0 / 120 + square * (-1.0 / 5040 + square * (1.0 / 362880))))
    )
    cosine = 1.0 + square * (
        -0.5
        + square
        * (1.0 / 24 + square * (-1.0 / 720 + square * (1.0 / 40320 - square * (1.0 / 3628800))))
    )
    swap = (quadrant & 1) == 1
    real = jnp.where(swap, sine, cosine)
    imaginary = jnp.where(swap, cosine, sine)
    real = jnp.where(((quadrant + 1) & 2) == 2, -real, real)
    imaginary = jnp.where((quadrant & 2) == 2, -imaginary, imaginary)
    return real, imaginary


def forward_kernel(waves, even, odd, fourier, table, *, slots, lon_count):
    dists, levs, parities, tall, _ = fourier.shape
    half = even.shape[1]
    scaling = 1.0 / math.sqrt(lon_count)

    @pl.when(pl.program_id(0) == 0)
    def _():
        fine = lax.broadcasted_iota(jnp.int32, (1, LANES), 1)
        for parity in range(parities):
            for dist in range(dists):
                wave = waves[dist, parity]
                c_step, s_step = cos_sin((wave * LANES) & (lon_count - 1), lon_count // 4)
                c_here, s_here = cos_sin((wave * fine) & (lon_count - 1), lon_count // 4)
                c_here, s_here = c_here * scaling, s_here * scaling
                for block in range(half // LANES):
                    there = slice(block * LANES, (block + 1) * LANES)
                    for part, value in enumerate((c_here, -s_here)):
                        value = value.astype(table.dtype)
                        for lev in range(levs):
                            top = (dist * levs + lev) * tall + part * slots
                            table[parity, top : top + slots, there] = value[
                                lev * slots : (lev + 1) * slots
                            ]
                    c_here, s_here = (
                        c_here * c_step - s_here * s_step,
                        s_here * c_step + c_here * s_step,
                    )

    for parity, grid_rows in enumerate((even, odd)):
        sums = lax.dot_general(
            table[parity],
            grid_rows[...],
            (((1,), (1,)), ((), ())),
            preferred_element_type=jnp.float32,
        ).astype(fourier.dtype)
        for dist in range(dists):
            for lev in range(levs):
                top = (dist * levs + lev) * tall
                fourier[dist, lev, parity] = sums[top : top + tall]


def forward_stage(waves, even, odd, slots, lon_count):
    dists, parities, lines, _ = waves.shape
    levs = lines // slots
    rows, half = even.shape
    block = min(rows, 512)
    whole = lambda shape: pl.BlockSpec(shape, lambda i: (0,) * len(shape))
    shape = (dists, levs, parities, 2 * slots, rows)
    table_shape = (parities, dists * levs * 2 * slots, half)
    return pl.pallas_call(
        functools.partial(forward_kernel, slots=slots, lon_count=lon_count),
        grid=(rows // block,),
        in_specs=[whole(waves.shape)] + [pl.BlockSpec((block, half), lambda i: (i, 0))] * 2,
        out_specs=[
            pl.BlockSpec(shape[:-1] + (block,), lambda i: (0, 0, 0, 0, i)),
            whole(table_shape),
        ],
        out_shape=[
            jax.ShapeDtypeStruct(shape, jnp.bfloat16),
            jax.ShapeDtypeStruct(table_shape, jnp.bfloat16),
        ],
        cost_estimate=pl.CostEstimate(
            flops=2 * math.prod(shape) * half,
            bytes_accessed=4 * rows * half + 2 * math.prod(shape) + 2 * math.prod(table_shape),
            transcendentals=0,
        ),
    )(waves, even, odd)


def inverse_kernel(*refs, dists, chunks):
    hemis, tables, out = refs[: dists * chunks], refs[dists * chunks : -1], refs[-1]
    half = tables[0].shape[2]
    sums = []
    for parity in range(2):
        total = None
        for chunk in range(chunks):
            hemi = jnp.concatenate(
                [
                    hemis[chunk * dists + dist][lev, parity]
                    for dist in range(dists)
                    for lev in range(hemis[0].shape[0])
                ],
                axis=0,
            )
            table = tables[chunk][parity]
            part = lax.dot_general(
                hemi, table, (((0,), (0,)), ((), ())), preferred_element_type=jnp.float32
            )
            total = part if total is None else total + part
        sums.append(total)
    out[:, :half] = (sums[0] + sums[1]).astype(out.dtype)
    out[:, half:] = (sums[0] - sums[1]).astype(out.dtype)


def inverse_stage(hemis, tables):
    rows = hemis[0][0].shape[-1]
    half = tables[0].shape[-1]
    dists = len(hemis[0])
    block = min(rows, 256)
    flat = [piece for pieces in hemis for piece in pieces]
    whole = lambda shape: pl.BlockSpec(shape, lambda i: (0,) * len(shape))
    total = sum(piece.size for piece in flat)
    return pl.pallas_call(
        functools.partial(inverse_kernel, dists=dists, chunks=len(hemis)),
        grid=(rows // block,),
        in_specs=[pl.BlockSpec(piece.shape[:3] + (block,), lambda i: (0, 0, 0, i)) for piece in flat]
        + [whole(table.shape) for table in tables],
        out_specs=pl.BlockSpec((block, 2 * half), lambda i: (i, 0)),
        out_shape=jax.ShapeDtypeStruct((rows, 2 * half), jnp.bfloat16),
        cost_estimate=pl.CostEstimate(
            flops=2 * total * half,
            bytes_accessed=2 * total + 2 * sum(t.size for t in tables) + 4 * rows * half,
            transcendentals=0,
        ),
    )(*flat, *tables)


def in_three(matrix):
    high = matrix.astype(jnp.bfloat16)
    low = (matrix - high.astype(jnp.float32)).astype(jnp.bfloat16)
    return jnp.concatenate([high, high, low], axis=1)


def legendre_kernel(
    numbers, *refs, lats, dists, lev_count, wave_count, slots, first_slot, lat_at, together
):
    near, far = refs[:dists], refs[dists : dists + lev_count - 1]
    table, analysis, synthesis, rate, out, work, lines_in = refs[dists + lev_count - 1 :]
    slots_all = lat_at
    slot = pl.program_id(0)
    tall = 2 * slots
    lines = out.shape[4] // lats
    group = lev_count * lines
    rows = 2 * group

    def piece(dist, parity, lev, line):
        there = slice(line * lats, (line + 1) * lats)
        if lev == 0:
            return near[dist][0, parity, :, there]
        return far[lev - 1][dist, parity, :, there]

    def place(dist, parity, lev, line):
        at = (((dist * 2 + parity) * lev_count + lev) * lines + line) * tall
        return slice(at, at + tall)

    every = [
        (dist, parity, lev, line)
        for dist in range(dists)
        for parity in range(2)
        for lev in range(lev_count)
        for line in range(lines)
    ]

    @pl.when(slot == 0)
    def _():
        for at in every:
            work[place(*at), :] = piece(*at).astype(jnp.float32)

    parity_here = numbers[3 * slots_all]
    lat_here = numbers[3 * slots_all + 1]
    cols = table.shape[3]
    column = lax.broadcasted_iota(jnp.int32, (1, cols), 1)
    lane = lax.broadcasted_iota(jnp.int32, (1, lats), 1)

    def rows_at(slot, block, parity, part):
        dist = block ^ lat_here
        at = (dist * 2 + parity) * (group * tall) + part * slots + slot
        return pl.ds(at, group, stride=tall)

    def starts_of(slot):
        at = first_slot + slot
        return [numbers[slots_all + at], numbers[2 * slots_all + at]]

    def gather(slot, lines_in):
        starts = starts_of(slot)
        for block in range(dists):
            for parity in range(2):
                keep = lane + block * lats >= starts[parity]
                for part in range(2):
                    value = work[rows_at(slot, block, parity, part), :]
                    top = parity * rows + part * group
                    lines_in[top : top + group, block * lats : (block + 1) * lats] = jnp.where(
                        keep, value, 0.0
                    ).astype(lines_in.dtype)

    def mix(matrix, value):
        high = value.astype(jnp.bfloat16)
        low = (value - high.astype(jnp.float32)).astype(jnp.bfloat16)
        return jnp.dot(
            matrix[...],
            jnp.concatenate([high, low, high], axis=0),
            preferred_element_type=jnp.float32,
        )

    def transform(slot, lines_in, legendre):
        first = numbers[first_slot + slot]
        second = wave_count - 1 - first
        first_odd = (first & 1) == 1
        count_one = ((wave_count - 1 - first - parity_here) >> 1) + 1
        count_two = jnp.maximum(((first - parity_here) >> 1) + 1, 0)
        degree = jnp.where(
            column < count_one,
            first + parity_here + 2 * column,
            second + parity_here + 2 * (column - count_one),
        )
        even_from = jnp.where(first_odd, count_one, 0)
        even_to = jnp.where(first_odd, count_one + count_two, count_one)
        odd_from = jnp.where(first_odd, 0, count_one)
        odd_to = jnp.where(first_odd, count_one, count_one + count_two)
        in_even = (column >= even_from) & (column < even_to)
        in_odd = (column >= odd_from) & (column < odd_to)
        both = jnp.dot(lines_in[...], legendre[...], preferred_element_type=jnp.float32)
        spectral = jnp.where(in_even, both[:rows], both[rows:])
        level_deg = degree.astype(jnp.float32)
        growth = level_deg * (level_deg + 1.0) / float(wave_count * wave_count)
        factor = 1.0 / (1.0 + growth * rate[...])
        mixed = mix(analysis, spectral).reshape(2, rows // 2, cols)
        coupled = mix(synthesis, (mixed * factor[None]).reshape(rows, cols))
        split = jnp.concatenate(
            [jnp.where(in_even, coupled, 0.0), jnp.where(in_odd, coupled, 0.0)], axis=0
        ).astype(jnp.bfloat16)
        return lax.dot_general(
            split, legendre[...], (((1,), (1,)), ((), ())), preferred_element_type=jnp.float32
        )

    def scatter(slot, back):
        starts = starts_of(slot)
        first = numbers[first_slot + slot]
        even_wave = jnp.where((first & 1) == 1, wave_count - 1 - first, first)
        weights = [jnp.where(even_wave == 0, 1.0, 2.0), 2.0]
        for block in range(dists):
            for parity in range(2):
                keep = lane + block * lats >= starts[parity]
                for part in range(2):
                    top = parity * rows + part * group
                    value = back[top : top + group, block * lats : (block + 1) * lats]
                    work[rows_at(slot, block, parity, part), :] = jnp.where(
                        keep, value * weights[parity], 0.0
                    )

    here = [slot * together + sub for sub in range(together)]
    for sub in range(together):
        gather(here[sub], lines_in.at[sub])
    backs = [transform(here[sub], lines_in.at[sub], table.at[sub, 0]) for sub in range(together)]
    for sub in range(together):
        scatter(here[sub], backs[sub])

    @pl.when(slot == slots // together - 1)
    def _():
        for at in every:
            dist, parity, lev, line = at
            out[lev, dist, parity, :, line * lats : (line + 1) * lats] = work[
                place(*at), :
            ].astype(out.dtype)


def legendre_stage(
    near, far, legendre, numbers, analysis, synthesis, rate, wave_count, lats, slots, first_slot
):
    dists, lev_count = len(near), len(far) + 1
    _, parities, tall, width = near[0].shape
    slots_all, _, lat_total, cols = legendre.shape
    rows = 2 * lev_count * (width // lats)
    together = 2 if slots % 2 == 0 and first_slot % 2 == 0 else 1
    whole = lambda shape: pl.BlockSpec(shape, lambda i, n: (0,) * len(shape))
    shape = (lev_count, dists, parities, tall, width)
    return pl.pallas_call(
        functools.partial(
            legendre_kernel,
            lats=lats,
            dists=dists,
            lev_count=lev_count,
            wave_count=wave_count,
            slots=slots,
            first_slot=first_slot,
            lat_at=slots_all,
            together=together,
        ),
        grid_spec=pltpu.PrefetchScalarGridSpec(
            num_scalar_prefetch=1,
            grid=(slots // together,),
            in_specs=[
                pl.BlockSpec((1, parities, tall, width), lambda i, n: (0, 0, 0, 0)) for _ in near
            ]
            + [whole(piece.shape) for piece in far]
            + [
                pl.BlockSpec(
                    (together, 1, lat_total, cols),
                    lambda i, n: (first_slot // together + i, 0, 0, 0),
                ),
                whole(analysis.shape),
                whole(synthesis.shape),
                whole(rate.shape),
            ],
            out_specs=whole(shape),
            scratch_shapes=[
                pltpu.VMEM((dists * rows * tall, lats), jnp.float32),
                pltpu.VMEM((together, 2 * rows, lat_total), jnp.bfloat16),
            ],
        ),
        out_shape=jax.ShapeDtypeStruct(shape, jnp.bfloat16),
        cost_estimate=pl.CostEstimate(
            flops=slots * (2 * 2 * 2 * rows * lat_total * cols + 2 * 2 * 3 * rows * rows * cols),
            bytes_accessed=slots * lat_total * cols * 2 + 4 * math.prod(shape),
            transcendentals=0,
        ),
    )(numbers, *near, *far, legendre, analysis, synthesis, rate)


def chunk_sizes(slots):
    return [slots // 4] * 4 if slots % 4 == 0 else [slots]


def local(grid_state, legendre, pair_order, band_start, mode_analysis, mode_synthesis, mode_rate):
    lat_count = lax.axis_size("lat")
    lev_count = lax.axis_size("lev")
    lat_here = lax.axis_index("lat")
    lev_here = lax.axis_index("lev")
    parity = lax.axis_index("fld")
    wave_count = band_start.shape[0]
    lon_count = grid_state.shape[-1]
    field_count, levels_here, _, lats_here, _ = grid_state.shape
    slots_here = legendre.shape[0]
    modes_count = mode_rate.shape[0]
    sizes = chunk_sizes(slots_here)
    firsts = [sum(sizes[:chunk]) for chunk in range(len(sizes))]

    indices, odds = [], []
    for first, slots in zip(firsts, sizes):
        shape = (lat_count, 2, lev_count, slots)
        axis = lambda k: lax.broadcasted_iota(jnp.int32, shape, k)
        owner = (axis(0) ^ lat_here) * lev_count + (axis(2) ^ lev_here)
        indices.append((owner * slots_here + first + axis(3)).reshape(-1))
        odds.append(axis(1).reshape(-1))
    pair_at = pick(pair_order, jnp.concatenate(indices))
    odd_at = jnp.concatenate(odds)
    all_waves = jnp.where((pair_at & 1) == odd_at, pair_at, wave_count - 1 - pair_at)
    all_waves = jnp.broadcast_to(all_waves[:, None], (all_waves.shape[0], LANES))

    own_first = lax.dynamic_slice_in_dim(
        pair_order, (lat_here * lev_count + lev_here) * slots_here, slots_here
    )
    first_is_odd = (own_first & 1) == 1
    even_wave = jnp.where(first_is_odd, wave_count - 1 - own_first, own_first)
    own_starts = pick(
        band_start, jnp.concatenate([even_wave, wave_count - 1 - even_wave])
    )
    numbers = jnp.concatenate(
        [own_first, own_starts, jnp.stack([parity, lat_here]).astype(jnp.int32)]
    )

    mode_at = (
        jnp.arange(field_count, dtype=jnp.int32)[None, :, None] * (lev_count * levels_here)
        + (jnp.arange(lev_count, dtype=jnp.int32) ^ lev_here)[:, None, None] * levels_here
        + jnp.arange(levels_here, dtype=jnp.int32)[None, None, :]
    ).reshape(-1)
    select = (
        jnp.arange(modes_count, dtype=jnp.int32)[:, None] == mode_at[None, :]
    ).astype(jnp.float32)
    exact = functools.partial(jnp.dot, precision=lax.Precision.HIGHEST)
    part_eye = jnp.eye(2, dtype=jnp.float32)
    analysis = in_three(jnp.kron(part_eye, exact(mode_analysis, select)))
    synthesis = in_three(jnp.kron(part_eye, exact(select.T, mode_synthesis)))
    rate = mode_rate[:, None]

    even, odd = folded_products(grid_state)
    sign_own = (1 - 2 * parity).astype(jnp.float32)

    def combine(partner, own):
        return (partner.astype(jnp.float32) + sign_own * own.astype(jnp.float32)).astype(
            jnp.bfloat16
        )

    tables, incoming = [], []
    for chunk, slots in enumerate(sizes):
        size = lat_count * 2 * lev_count * slots
        at = lat_count * 2 * lev_count * firsts[chunk]
        waves = all_waves[at : at + size].reshape(lat_count, 2, -1, LANES)
        fourier, table = forward_stage(waves, even, odd, slots, lon_count)
        tables.append(table)
        mirror = swap_with(fourier, "fld", 1)
        near = [combine(mirror[dist], fourier[dist]) for dist in range(lat_count)]
        near = [swap_with(piece, "lat", dist) for dist, piece in enumerate(near)]
        far = [
            swap_with(jnp.stack([block[dist] for block in near]), "lev", dist)
            for dist in range(1, lev_count)
        ]
        incoming.append((near, far))
    hemis = []
    for chunk, slots in enumerate(sizes):
        returned = legendre_stage(
            *incoming[chunk],
            legendre,
            numbers,
            analysis,
            synthesis,
            rate,
            wave_count,
            lats_here,
            slots,
            firsts[chunk],
        )
        partner = swap_with(returned, "fld", 1)
        arrived = [
            swap_with(combine(partner[dist], returned[dist]), "lev", dist)
            for dist in range(lev_count)
        ]
        hemis.append(
            [
                swap_with(jnp.stack([block[dist] for block in arrived]), "lat", dist)
                for dist in range(lat_count)
            ]
        )
    grid_out = inverse_stage(hemis, tables)
    return grid_out.reshape(field_count, levels_here, 1, lats_here, lon_count)


def solution(mesh):
    return jax.shard_map(
        local,
        mesh=mesh,
        in_specs=(
            P("member", "lev", "fld", "lat", None),
            P(("lat", "lev"), "fld", None, None),
            P(),
            P(),
            P(),
            P(),
            P(),
        ),
        out_specs=P("member", "lev", "fld", "lat", None),
        check_vma=False,
    )
```

```python
import functools
import math

import jax
import jax.numpy as jnp
from jax import lax
from jax.experimental import pallas as pl
from jax.experimental.pallas import tpu as pltpu
from jax.sharding import PartitionSpec as P


LANES = 128
VMEM_LIMIT = 16 << 20


def swap_with(value, axis, mask, near=True):
    if mask == 0:
        return value
    pairs = [(source, source ^ mask) for source in range(lax.axis_size(axis))]
    value = lax.ppermute(value, axis, pairs)
    return pltpu.with_memory_space_constraint(value, pltpu.VMEM) if near else value


def pick(table, index):
    places = jnp.arange(table.shape[0], dtype=jnp.int32)
    return jnp.sum(jnp.where(index[:, None] == places[None, :], table[None, :], 0), axis=1)


def fold_kernel(sign, own, mirror, even, odd):
    half = even.shape[2]
    lats = even.shape[1]
    step = 16 if lats % 16 == 0 else lats

    def products(state, rows, columns):
        wind_part, heat_part = state[0, 0, 0, rows, columns], state[1, 0, 0, rows, columns]
        wind, heat = wind_part.astype(jnp.float32), heat_part.astype(jnp.float32)
        return wind_part * heat_part, (wind * wind - heat * heat).astype(jnp.bfloat16)

    sign_own = sign[0].astype(jnp.float32).astype(jnp.bfloat16)
    for top in range(0, lats, step):
        rows = slice(top, top + step)
        for left in range(0, half, LANES):
            columns = slice(left, left + LANES)
            pieces = [
                [
                    (
                        products(mirror, rows, there),
                        [value * sign_own for value in products(own, rows, there)],
                    )
                    for there in (columns, slice(half + left, half + left + LANES))
                ]
            ][0]
            for field in range(2):
                low, high = [
                    there[field].astype(jnp.float32) + here[field].astype(jnp.float32)
                    for there, here in pieces
                ]
                even[field, rows, columns] = (low + high).astype(even.dtype)
                odd[field, rows, columns] = (low - high).astype(odd.dtype)


def folded_products(grid_state, mirror, sign_own):
    fields, levels, _, lats, lon_count = grid_state.shape
    half = lon_count // 2
    out = jax.ShapeDtypeStruct((fields, levels * lats, half), jnp.bfloat16)
    state = pl.BlockSpec((fields, 1, 1, lats, lon_count), lambda i, n: (0, i, 0, 0, 0))
    even, odd = pl.pallas_call(
        fold_kernel,
        grid_spec=pltpu.PrefetchScalarGridSpec(
            num_scalar_prefetch=1,
            grid=(levels,),
            in_specs=[state] * 2,
            out_specs=[pl.BlockSpec((fields, lats, half), lambda i, n: (0, i, 0))] * 2,
        ),
        out_shape=[out, out],
        compiler_params=pltpu.CompilerParams(vmem_limit_bytes=VMEM_LIMIT),
        cost_estimate=pl.CostEstimate(
            flops=grid_state.size * 8, bytes_accessed=grid_state.size * 6, transcendentals=0
        ),
    )(sign_own[None], grid_state, mirror)
    return even.reshape(-1, half), odd.reshape(-1, half)


def cos_sin(phase, quarter):
    shift = quarter.bit_length() - 1
    quadrant = (phase + quarter // 2) >> shift
    theta = (phase - (quadrant << shift)).astype(jnp.float32) * (0.5 * math.pi / quarter)
    square = theta * theta
    sine = theta * (
        1.0
        + square
        * (-1.0 / 6 + square * (1.0 / 120 + square * (-1.0 / 5040 + square * (1.0 / 362880))))
    )
    cosine = 1.0 + square * (
        -0.5
        + square
        * (1.0 / 24 + square * (-1.0 / 720 + square * (1.0 / 40320 - square * (1.0 / 3628800))))
    )
    swap = (quadrant & 1) == 1
    real = jnp.where(swap, sine, cosine)
    imaginary = jnp.where(swap, cosine, sine)
    real = jnp.where(((quadrant + 1) & 2) == 2, -real, real)
    imaginary = jnp.where((quadrant & 2) == 2, -imaginary, imaginary)
    return real, imaginary


def forward_kernel(waves, even, odd, *outs, slots, lon_count):
    fourier, table = outs[:-1], outs[-1]
    dists = len(fourier)
    levs, parities, tall, _ = fourier[0].shape
    half = even.shape[1]
    scaling = 1.0 / math.sqrt(lon_count)

    @pl.when(pl.program_id(0) == 0)
    def _():
        fine = lax.broadcasted_iota(jnp.int32, (1, LANES), 1)
        for parity in range(parities):
            for dist in range(dists):
                wave = waves[0, dist, parity]
                c_step, s_step = cos_sin((wave * LANES) & (lon_count - 1), lon_count // 4)
                c_here, s_here = cos_sin((wave * fine) & (lon_count - 1), lon_count // 4)
                c_here, s_here = c_here * scaling, s_here * scaling
                for block in range(half // LANES):
                    there = slice(block * LANES, (block + 1) * LANES)
                    for part, value in enumerate((c_here, -s_here)):
                        value = value.astype(table.dtype)
                        for lev in range(levs):
                            top = (dist * levs + lev) * tall + part * slots
                            table[parity, top : top + slots, there] = value[
                                lev * slots : (lev + 1) * slots
                            ]
                    c_here, s_here = (
                        c_here * c_step - s_here * s_step,
                        s_here * c_step + c_here * s_step,
                    )

    for parity, grid_rows in enumerate((even, odd)):
        sums = lax.dot_general(
            table[parity],
            grid_rows[...],
            (((1,), (1,)), ((), ())),
            preferred_element_type=jnp.float32,
        ).astype(table.dtype)
        for dist in range(dists):
            for lev in range(levs):
                top = (dist * levs + lev) * tall
                fourier[dist][lev, parity] = sums[top : top + tall]


def forward_stage(waves, chunk, even, odd, slots, lon_count):
    _, dists, parities, lines, _ = waves.shape
    levs = lines // slots
    rows, half = even.shape
    block = min(rows, 512)
    whole = lambda shape: pl.BlockSpec(shape, lambda i: (0,) * len(shape))
    shape = (levs, parities, 2 * slots, rows)
    table_shape = (parities, dists * levs * 2 * slots, half)
    return pl.pallas_call(
        functools.partial(forward_kernel, slots=slots, lon_count=lon_count),
        grid=(rows // block,),
        in_specs=[pl.BlockSpec((1,) + waves.shape[1:], lambda i: (chunk, 0, 0, 0, 0))]
        + [pl.BlockSpec((block, half), lambda i: (i, 0))] * 2,
        out_specs=[pl.BlockSpec(shape[:-1] + (block,), lambda i: (0, 0, 0, i))] * dists
        + [whole(table_shape)],
        out_shape=[jax.ShapeDtypeStruct(shape, jnp.bfloat16)] * dists
        + [pltpu.HBM(table_shape, jnp.bfloat16)],
        compiler_params=pltpu.CompilerParams(vmem_limit_bytes=VMEM_LIMIT),
        cost_estimate=pl.CostEstimate(
            flops=2 * dists * math.prod(shape) * half,
            bytes_accessed=4 * rows * half + 4 * math.prod(table_shape),
            transcendentals=0,
        ),
    )(waves, even, odd)


def inverse_kernel(*refs, levs, dists, chunks, first, last):
    count = levs + dists - 1
    hemis, rest = refs[: count * chunks], refs[count * chunks :]
    tables, before, out = rest[:chunks], rest[chunks:-1], rest[-1]
    half = tables[0].shape[2]
    sums = []
    for parity in range(2):
        total = None if first else before[0][parity]
        for chunk in range(chunks):
            pieces = hemis[chunk * count : (chunk + 1) * count]
            hemi = jnp.concatenate(
                [piece[0, parity] for piece in pieces[:levs]]
                + [piece[lev, parity] for piece in pieces[levs:] for lev in range(levs)],
                axis=0,
            )
            part = lax.dot_general(
                hemi,
                tables[chunk][parity],
                (((0,), (0,)), ((), ())),
                preferred_element_type=jnp.float32,
            )
            total = part if total is None else total + part
        sums.append(total)
    if last:
        out[:, :half] = (sums[0] + sums[1]).astype(out.dtype)
        out[:, half:] = (sums[0] - sums[1]).astype(out.dtype)
    else:
        out[0], out[1] = sums


def inverse_stage(hemis, tables, before, last):
    rows = hemis[0][0][0].shape[-1]
    half = tables[0].shape[-1]
    levs, dists = len(hemis[0][0]), len(hemis[0][1]) + 1
    block = min(rows, 256)
    flat, specs = [], []
    for near, far in hemis:
        flat += near + far
        at = lambda i: (0, 0, 0, i)
        specs += [pl.BlockSpec((1,) + piece.shape[1:3] + (block,), at) for piece in near]
        specs += [pl.BlockSpec(piece.shape[:3] + (block,), at) for piece in far]
    whole = lambda shape: pl.BlockSpec(shape, lambda i: (0,) * len(shape))
    total = sum(table.size // half for table in tables) * rows
    sums = pl.BlockSpec((2, block, half), lambda i: (0, i, 0))
    if last:
        out_spec = pl.BlockSpec((block, 2 * half), lambda i: (i, 0))
        out_shape = jax.ShapeDtypeStruct((rows, 2 * half), jnp.bfloat16)
    else:
        out_spec = sums
        out_shape = jax.ShapeDtypeStruct((2, rows, half), jnp.float32)
    return pl.pallas_call(
        functools.partial(
            inverse_kernel,
            levs=levs,
            dists=dists,
            chunks=len(hemis),
            first=before is None,
            last=last,
        ),
        grid=(rows // block,),
        in_specs=specs
        + [whole(table.shape) for table in tables]
        + [sums] * (before is not None),
        out_specs=out_spec,
        out_shape=out_shape,
        compiler_params=pltpu.CompilerParams(vmem_limit_bytes=VMEM_LIMIT),
        cost_estimate=pl.CostEstimate(
            flops=2 * total * half,
            bytes_accessed=2 * total + 2 * sum(t.size for t in tables) + 8 * rows * half,
            transcendentals=0,
        ),
    )(*flat, *tables, *([] if before is None else [before]))


def regroup_kernel(*refs):
    *refs, arrived = refs
    count = refs[0].shape[0]
    pieces, outs = refs[: len(refs) - count + 1], refs[len(refs) - count + 1 :]
    copies = [
        pltpu.make_async_copy(piece.at[index + 1], out.at[source], arrived.at[index, source])
        for index, out in enumerate(outs)
        for source, piece in enumerate(pieces)
    ]
    for copy in copies:
        copy.start()
    for copy in copies:
        copy.wait()


def regroup(pieces):
    count, rest = pieces[0].shape[0], pieces[0].shape[1:]
    size = pieces[0].dtype.itemsize * math.prod(rest) * len(pieces) * (count - 1)
    return pl.pallas_call(
        regroup_kernel,
        in_specs=[pl.BlockSpec(memory_space=pl.ANY)] * len(pieces),
        out_shape=[jax.ShapeDtypeStruct((len(pieces),) + rest, pieces[0].dtype)] * (count - 1),
        scratch_shapes=[pltpu.SemaphoreType.DMA((count - 1, len(pieces)))],
        compiler_params=pltpu.CompilerParams(vmem_limit_bytes=VMEM_LIMIT),
        cost_estimate=pl.CostEstimate(flops=0, bytes_accessed=2 * size, transcendentals=0),
    )(*pieces)


def in_three(matrix):
    high = matrix.astype(jnp.bfloat16)
    low = (matrix - high.astype(jnp.float32)).astype(jnp.bfloat16)
    return jnp.concatenate([high, high, low], axis=1)


def legendre_kernel(
    numbers, *refs, lats, dists, lev_count, wave_count, slots, first_slot, lat_at, together
):
    near, far = refs[:dists], refs[dists : dists + lev_count - 1]
    table, analysis, synthesis, rate, out, work, lines_in, pieces, arrived = refs[
        dists + lev_count - 1 :
    ]
    slots_all = lat_at
    slot = pl.program_id(0)
    tall = 2 * slots
    lines = out.shape[4] // lats
    group = lev_count * lines
    rows = 2 * group

    def piece(dist, parity, lev, line):
        return pieces[lev, dist, parity, :, line * lats : (line + 1) * lats]

    def place(dist, parity, lev, line):
        at = (((dist * 2 + parity) * lev_count + lev) * lines + line) * tall
        return slice(at, at + tall)

    every = [
        (dist, parity, lev, line)
        for dist in range(dists)
        for parity in range(2)
        for lev in range(lev_count)
        for line in range(lines)
    ]

    @pl.when(slot == 0)
    def _():
        copies = [
            pltpu.make_async_copy(ref.at[0], pieces.at[0, dist], arrived.at[dist])
            for dist, ref in enumerate(near)
        ] + [
            pltpu.make_async_copy(ref, pieces.at[lev + 1], arrived.at[dists + lev])
            for lev, ref in enumerate(far)
        ]
        for copy in copies:
            copy.start()
        for copy in copies:
            copy.wait()
        for at in every:
            work[place(*at), :] = piece(*at).astype(jnp.float32)

    parity_here = numbers[3 * slots_all]
    lat_here = numbers[3 * slots_all + 1]
    cols = table.shape[3]
    column = lax.broadcasted_iota(jnp.int32, (1, cols), 1)
    lane = lax.broadcasted_iota(jnp.int32, (1, lats), 1)
    modes = rate.shape[1]
    across = lax.broadcasted_iota(jnp.int32, (modes, modes), 1)
    down = lax.broadcasted_iota(jnp.int32, (modes, modes), 0)
    rates = jnp.sum(jnp.where(across == down, rate[...], 0.0), axis=1, keepdims=True)

    def rows_at(slot, block, parity, part):
        dist = block ^ lat_here
        at = (dist * 2 + parity) * (group * tall) + part * slots + slot
        return pl.ds(at, group, stride=tall)

    def starts_of(slot):
        at = first_slot + slot
        return [numbers[slots_all + at], numbers[2 * slots_all + at]]

    def gather(slot, lines_in):
        starts = starts_of(slot)
        for block in range(dists):
            for parity in range(2):
                keep = lane + block * lats >= starts[parity]
                for part in range(2):
                    value = work[rows_at(slot, block, parity, part), :]
                    top = parity * rows + part * group
                    lines_in[top : top + group, block * lats : (block + 1) * lats] = jnp.where(
                        keep, value, 0.0
                    ).astype(lines_in.dtype)

    def parts_of(value):
        high = value.astype(jnp.bfloat16)
        low = (value - high.astype(jnp.float32)).astype(jnp.bfloat16)
        return jnp.concatenate([high, low, high], axis=0)

    def mix(matrix, parts):
        return jnp.dot(matrix[...], parts, preferred_element_type=jnp.float32)

    def transform(slot, lines_in, legendre):
        first = numbers[first_slot + slot]
        second = wave_count - 1 - first
        first_odd = (first & 1) == 1
        count_one = ((wave_count - 1 - first - parity_here) >> 1) + 1
        count_two = jnp.maximum(((first - parity_here) >> 1) + 1, 0)
        both = jnp.dot(lines_in[...], legendre[...], preferred_element_type=jnp.float32)
        yield
        degree = jnp.where(
            column < count_one,
            first + parity_here + 2 * column,
            second + parity_here + 2 * (column - count_one),
        )
        even_from = jnp.where(first_odd, count_one, 0)
        even_to = jnp.where(first_odd, count_one + count_two, count_one)
        odd_from = jnp.where(first_odd, 0, count_one)
        odd_to = jnp.where(first_odd, count_one, count_one + count_two)
        in_even = (column >= even_from) & (column < even_to)
        in_odd = (column >= odd_from) & (column < odd_to)
        parts = parts_of(jnp.where(in_even, both[:rows], both[rows:]))
        yield
        mixed = mix(analysis, parts).reshape(2, rows // 2, cols)
        yield
        level_deg = degree.astype(jnp.float32)
        growth = level_deg * (level_deg + 1.0) / float(wave_count * wave_count)
        factor = 1.0 / (1.0 + growth * rates)
        parts = parts_of((mixed * factor[None]).reshape(rows, cols))
        yield
        coupled = mix(synthesis, parts)
        yield
        split = jnp.concatenate(
            [jnp.where(in_even, coupled, 0.0), jnp.where(in_odd, coupled, 0.0)], axis=0
        ).astype(jnp.bfloat16)
        yield
        back = lax.dot_general(
            split, legendre[...], (((1,), (1,)), ((), ())), preferred_element_type=jnp.float32
        )
        yield
        scatter(slot, back)

    def scatter(slot, back):
        starts = starts_of(slot)
        first = numbers[first_slot + slot]
        even_wave = jnp.where((first & 1) == 1, wave_count - 1 - first, first)
        weights = [jnp.where(even_wave == 0, 1.0, 2.0), 2.0]
        for block in range(dists):
            for parity in range(2):
                keep = lane + block * lats >= starts[parity]
                for part in range(2):
                    top = parity * rows + part * group
                    value = back[top : top + group, block * lats : (block + 1) * lats]
                    work[rows_at(slot, block, parity, part), :] = jnp.where(
                        keep, value * weights[parity], 0.0
                    )

    here = [slot * together + sub for sub in range(together)]
    for sub in range(together):
        gather(here[sub], lines_in.at[sub])
    chains = [transform(here[sub], lines_in.at[sub], table.at[sub, 0]) for sub in range(together)]
    done = object()
    while any([next(chain, done) is not done for chain in chains]):
        pass

    @pl.when(slot == slots // together - 1)
    def _():
        for at in every:
            dist, parity, lev, line = at
            out[lev, dist, parity, :, line * lats : (line + 1) * lats] = work[
                place(*at), :
            ].astype(out.dtype)


def legendre_stage(
    near, far, legendre, numbers, analysis, synthesis, rate, wave_count, lats, slots, first_slot
):
    dists, lev_count = len(near), len(far) + 1
    _, parities, tall, width = near[0].shape
    slots_all, _, lat_total, cols = legendre.shape
    rows = 2 * lev_count * (width // lats)
    together = 2 if slots % 2 == 0 and first_slot % 2 == 0 else 1
    whole = lambda shape: pl.BlockSpec(shape, lambda i, n: (0,) * len(shape))
    shape = (lev_count, dists, parities, tall, width)
    return pl.pallas_call(
        functools.partial(
            legendre_kernel,
            lats=lats,
            dists=dists,
            lev_count=lev_count,
            wave_count=wave_count,
            slots=slots,
            first_slot=first_slot,
            lat_at=slots_all,
            together=together,
        ),
        grid_spec=pltpu.PrefetchScalarGridSpec(
            num_scalar_prefetch=1,
            grid=(slots // together,),
            in_specs=[pl.BlockSpec(memory_space=pl.ANY)] * (len(near) + len(far))
            + [
                pl.BlockSpec(
                    (together, 1, lat_total, cols),
                    lambda i, n: (first_slot // together + i, 0, 0, 0),
                ),
                whole(analysis.shape),
                whole(synthesis.shape),
                whole(rate.shape),
            ],
            out_specs=whole(shape),
            scratch_shapes=[
                pltpu.VMEM((dists * rows * tall, lats), jnp.float32),
                pltpu.VMEM((together, 2 * rows, lat_total), jnp.bfloat16),
                pltpu.VMEM(shape, jnp.bfloat16),
                pltpu.SemaphoreType.DMA((len(near) + len(far),)),
            ],
        ),
        out_shape=jax.ShapeDtypeStruct(shape, jnp.bfloat16),
        compiler_params=pltpu.CompilerParams(vmem_limit_bytes=VMEM_LIMIT),
        cost_estimate=pl.CostEstimate(
            flops=slots * (2 * 2 * 2 * rows * lat_total * cols + 2 * 2 * 3 * rows * rows * cols),
            bytes_accessed=slots * lat_total * cols * 2 + 4 * math.prod(shape),
            transcendentals=0,
        ),
    )(numbers, *near, *far, legendre, analysis, synthesis, rate)


def chunk_sizes(slots):
    return [slots // 4] * 4 if slots % 4 == 0 else [slots]


def local(grid_state, legendre, pair_order, band_start, mode_analysis, mode_synthesis, mode_rate):
    lat_count = lax.axis_size("lat")
    lev_count = lax.axis_size("lev")
    lat_here = lax.axis_index("lat")
    lev_here = lax.axis_index("lev")
    parity = lax.axis_index("fld")
    wave_count = band_start.shape[0]
    lon_count = grid_state.shape[-1]
    field_count, levels_here, _, lats_here, _ = grid_state.shape
    slots_here = legendre.shape[0]
    modes_count = mode_rate.shape[0]
    sizes = chunk_sizes(slots_here)
    firsts = [sum(sizes[:chunk]) for chunk in range(len(sizes))]

    indices, odds = [], []
    for first, slots in zip(firsts, sizes):
        shape = (lat_count, 2, lev_count, slots)
        axis = lambda k: lax.broadcasted_iota(jnp.int32, shape, k)
        owner = (axis(0) ^ lat_here) * lev_count + (axis(2) ^ lev_here)
        indices.append((owner * slots_here + first + axis(3)).reshape(-1))
        odds.append(axis(1).reshape(-1))
    pair_at = pick(pair_order, jnp.concatenate(indices))
    odd_at = jnp.concatenate(odds)
    all_waves = jnp.where((pair_at & 1) == odd_at, pair_at, wave_count - 1 - pair_at)
    all_waves = jnp.broadcast_to(all_waves[:, None], (all_waves.shape[0], LANES)).reshape(
        len(sizes), lat_count, 2, -1, LANES
    )

    own_first = lax.dynamic_slice_in_dim(
        pair_order, (lat_here * lev_count + lev_here) * slots_here, slots_here
    )
    first_is_odd = (own_first & 1) == 1
    even_wave = jnp.where(first_is_odd, wave_count - 1 - own_first, own_first)
    own_starts = pick(
        band_start, jnp.concatenate([even_wave, wave_count - 1 - even_wave])
    )
    numbers = jnp.concatenate(
        [own_first, own_starts, jnp.stack([parity, lat_here]).astype(jnp.int32)]
    )

    mode_at = (
        jnp.arange(field_count, dtype=jnp.int32)[None, :, None] * (lev_count * levels_here)
        + (jnp.arange(lev_count, dtype=jnp.int32) ^ lev_here)[:, None, None] * levels_here
        + jnp.arange(levels_here, dtype=jnp.int32)[None, None, :]
    ).reshape(-1)
    select = (
        jnp.arange(modes_count, dtype=jnp.int32)[:, None] == mode_at[None, :]
    ).astype(jnp.float32)
    exact = functools.partial(jnp.dot, precision=lax.Precision.HIGHEST)
    part_eye = jnp.eye(2, dtype=jnp.float32)
    analysis = in_three(jnp.kron(part_eye, exact(mode_analysis, select)))
    synthesis = in_three(jnp.kron(part_eye, exact(select.T, mode_synthesis)))
    rate = mode_rate[None, :]

    sign_own = (1 - 2 * parity).astype(jnp.float32)
    mirror = swap_with(grid_state, "fld", 1, False)
    mirror, numbers, analysis, synthesis, all_waves = lax.optimization_barrier(
        (mirror, numbers, analysis, synthesis, all_waves)
    )
    grid_state = pltpu.with_memory_space_constraint(grid_state, pltpu.HBM)
    even, odd = folded_products(grid_state, mirror, 1 - 2 * parity)

    def combine(partner, own):
        return (partner.astype(jnp.float32) + sign_own * own.astype(jnp.float32)).astype(
            jnp.bfloat16
        )

    legendre = pltpu.with_memory_space_constraint(legendre, pltpu.HBM)
    tables, incoming = [], []
    for chunk, slots in enumerate(sizes):
        *near, table = forward_stage(all_waves, chunk, even, odd, slots, lon_count)
        tables.append(pltpu.with_memory_space_constraint(table, pltpu.HBM))
        near = [swap_with(piece, "lat", dist) for dist, piece in enumerate(near)]
        far = regroup(near)
        far = [swap_with(piece, "lev", dist + 1) for dist, piece in enumerate(far)]
        incoming.append((near, far))
    hemis = []
    for chunk, slots in enumerate(sizes):
        returned = legendre_stage(
            *incoming[chunk],
            legendre,
            numbers,
            analysis,
            synthesis,
            rate,
            wave_count,
            lats_here,
            slots,
            firsts[chunk],
        )
        partner = swap_with(returned, "fld", 1, False)
        arrived = [combine(partner[dist], returned[dist]) for dist in range(lev_count)]
        arrived = [swap_with(piece, "lev", dist) for dist, piece in enumerate(arrived)]
        far = regroup(arrived)
        far = [swap_with(piece, "lat", dist + 1) for dist, piece in enumerate(far)]
        hemis.append((arrived, far))
    sums = None
    if len(hemis) > 1:
        sums = inverse_stage(hemis[:-1], tables[:-1], None, False)
    grid_out = inverse_stage(hemis[-1:], tables[-1:], sums, True)
    return grid_out.reshape(field_count, levels_here, 1, lats_here, lon_count)


def solution(mesh):
    return jax.shard_map(
        local,
        mesh=mesh,
        in_specs=(
            P("member", "lev", "fld", "lat", None),
            P(("lat", "lev"), "fld", None, None),
            P(),
            P(),
            P(),
            P(),
            P(),
        ),
        out_specs=P("member", "lev", "fld", "lat", None),
        check_vma=False,
    )
```
